32 devices in a mesh: ctx: 16 (over z, x, core), ch: 2 (over y).
Axes of the slice: x: 2, y: 2, z: 4, core: 2. Of those that a mesh axis runs over, the one named last changes fastest.
Arguments:
- inputs: bfloat16 [8192, 4096], P('ctx', 'ch'), may hold values from -6 to 6
- proj_weight: bfloat16 [2, 4096, 128], P(None, 'ch'), may hold values from -0.09375 to 0.09375
- filters: float32 [128, 8192], P('ch', 'ctx'), may hold values from -1.5 to 1.5
- skip_gain: float32 [128], P('ch'), may hold values from 0.3 to 1.7
- targets: float32 [128, 8192], P('ch', 'ctx'), may hold values from -6 to 6
Outputs:
- outputs: float32 [128, 8192], P('ch', 'ctx')
- grad_inputs: float32 [8192, 4096], P('ctx', 'ch')
- grad_filter: float32 [128, 8192], P('ch', 'ctx')
- grad_proj: float32 [256, 4096], P('ctx', 'ch')
The draws below stay inside these ranges and needn't reach their ends.
All inputs are finite; a program needn't handle non-finite values.
Results may differ from the reference program's by a relative error of at most 0.0005.
Values sent between devices are 32-bit elements; how exact they have to be, the bound alone decides.
A program may use at most 64 MiB of HBM per device.

```python
import jax
import jax.numpy as jnp
from jax import lax

D = 4096
C = 128
SEQ = 8192


def draw_filters(key, part):
    key_list = jax.random.split(key, 6)
    position_grid = jnp.arange(SEQ).astype(jnp.float32)[None, :]
    chooser = jax.random.randint(key_list[0], (C, 1), 0, 8)
    slow_rate = jnp.exp(jax.random.uniform(key_list[1], (C, 1), minval=jnp.log(0.3 / SEQ), maxval=jnp.log(2.0 / SEQ)))
    fast_rate = jnp.exp(jax.random.uniform(key_list[2], (C, 1), minval=jnp.log(1.0 / 600.0), maxval=jnp.log(1.0 / 30.0)))
    rates = jnp.where(chooser < 4, slow_rate, fast_rate)
    roughness = jax.random.truncated_normal(key_list[3], -5.0, 5.0, (C, SEQ))
    decay_window = jnp.exp(-rates * position_grid)
    dropped_places = jax.random.randint(key_list[4], (C, 4), 0, SEQ)
    dropped_lengths = jax.random.uniform(key_list[5], (C, 4), minval=0.5, maxval=0.8)
    for spike_train in range(4):
        current_place = dropped_places[:, spike_train:spike_train + 1].astype(jnp.float32)
        decay_window = decay_window * jnp.where(position_grid >= current_place, dropped_lengths[:, spike_train:spike_train + 1], 1.0)
    amplitude = jnp.sqrt((1.0 - jnp.exp(-2.0 * rates)) / (1.0 - jnp.exp(-2.0 * rates * SEQ)))
    return (roughness * decay_window * amplitude).astype(jnp.float32)


def block_scale(own_key, dims, cuts, smallest, top_value):
    factor_of, own = 1.0, jax.random.fold_in(own_key, 6)
    for position, blocks in cuts:
        draws = jnp.exp(jax.random.uniform(jax.random.fold_in(own, position), (blocks,), jnp.float32, smallest / len(cuts), top_value / len(cuts)))
        factor_of = factor_of * jnp.repeat(draws, dims[position] // blocks).reshape([-1 if axis == position else 1 for axis in range(len(dims))])
    return factor_of


def bell_draw(own_key, extent, spread, limit, pieces=(), dtype=jnp.bfloat16):
    loudness = block_scale(own_key, extent, pieces, -0.22, 0.18) if pieces else 1.0
    values = jax.random.normal(own_key, extent, jnp.float32) * spread * loudness
    return jnp.minimum(jnp.maximum(values, -limit), limit).astype(dtype)


def setup_inputs(seed: int = 0) -> dict:
    keys = jax.random.split(jax.random.key(seed), 6)
    inputs = bell_draw(keys[0], (SEQ, D), 1.0, 6.0, ((0, 16), (1, 2)))
    proj_weight = bell_draw(keys[1], (2, D, C), D ** -0.5, 0.09375, ((1, 2),))
    filters = draw_filters(jax.random.fold_in(keys[5], 71), 0)
    skip_gain = jnp.clip(0.3 + 1.40000004 * jax.random.uniform(keys[3], (C,), jnp.float32) ** block_scale(keys[3], (C,), ((0, 2),), -0.2, 0.2), 0.3, 1.7)
    targets = bell_draw(keys[4], (C, SEQ), 1.0, 6.0, ((0, 2), (1, 16)), jnp.float32)
    return dict(inputs=inputs, proj_weight=proj_weight, filters=filters, skip_gain=skip_gain, targets=targets)


def reference(inputs, proj_weight, filters, skip_gain, targets):
    length_all = inputs.shape[0]
    padded = 2 * length_all
    scaling = float(length_all) ** -0.5
    flat_weight = jnp.transpose(proj_weight, (1, 0, 2)).reshape(D, 2 * C)
    projected = jnp.dot(inputs, flat_weight, preferred_element_type=jnp.float32)
    values = projected[:, :C].T
    gates = projected[:, C:].T
    value_freq = jnp.fft.rfft(values, n=padded, axis=1)
    filter_freq = jnp.fft.rfft(filters, n=padded, axis=1)
    skip_rows = skip_gain[:, None]
    conv = jnp.fft.irfft(value_freq * filter_freq, n=padded, axis=1)[:, :length_all] + skip_rows * values
    outputs = gates * conv
    residual = outputs - targets
    grad_conv = residual * gates
    grad_gate = residual * conv
    grad_freq = jnp.fft.rfft(grad_conv, n=padded, axis=1)
    grad_value = jnp.fft.irfft(grad_freq * jnp.conj(filter_freq), n=padded, axis=1)[:, :length_all] + skip_rows * grad_conv
    grad_filter = jnp.fft.irfft(grad_freq * jnp.conj(value_freq), n=padded, axis=1)[:, :length_all] * scaling
    grad_pair = jnp.concatenate([grad_value, grad_gate], 0).astype(jnp.float32)
    inputs_wide = inputs.astype(jnp.float32)
    grad_proj = jnp.dot(grad_pair, inputs_wide, precision=lax.Precision.HIGHEST, preferred_element_type=jnp.float32) * scaling
    weight_rows = jnp.transpose(proj_weight, (0, 2, 1)).reshape(2 * C, D).astype(jnp.float32)
    grad_inputs = jnp.dot(grad_pair.T, weight_rows, precision=lax.Precision.HIGHEST, preferred_element_type=jnp.float32)
    return outputs, grad_inputs, grad_filter, grad_proj
```

```python
import math

import functools

import jax
import jax.numpy as jnp
import numpy as np
from jax import lax
from jax.experimental import pallas as pl
from jax.experimental.pallas import tpu as pltpu
from jax.sharding import PartitionSpec as P

HIGHEST = lax.Precision.HIGHEST


def product(left, right):
    return jnp.dot(left, right, precision=HIGHEST, preferred_element_type=jnp.float32)


def angle_table(row_total, col_total, period):
    row_index = lax.broadcasted_iota(jnp.int32, (row_total, col_total), 0)
    col_index = lax.broadcasted_iota(jnp.int32, (row_total, col_total), 1)
    phase_index = row_index * col_index % period
    angles = 2.0 * math.pi / period * phase_index.astype(jnp.float32)
    return (jnp.cos(angles), jnp.sin(angles), row_index, col_index)


def twiddle(real_part, imag_part, frequencies, padded, direction):
    frames = real_part.shape[-1]
    offsets = lax.broadcasted_iota(jnp.int32, (2, frames), 1)
    phase_index = frequencies[:, None] * offsets % padded
    angles = direction * 2.0 * math.pi / padded * phase_index.astype(jnp.float32)
    cosine = jnp.cos(angles)[:, None, None, :]
    sine_table = jnp.sin(angles)[:, None, None, :]
    return (
        real_part * cosine - imag_part * sine_table,
        real_part * sine_table + imag_part * cosine,
    )


def multiply(left_real, left_imag, right_real, right_imag, conj_sign):
    right_imag = conj_sign * right_imag
    return (
        left_real * right_real - left_imag * right_imag,
        left_real * right_imag + left_imag * right_real,
    )


def to_blocks(fields_seq):
    return lax.all_to_all(fields_seq[None], "ctx", split_axis=3, concat_axis=0, tiled=True)


def to_frames(block_grouped):
    return lax.all_to_all(block_grouped, "ctx", split_axis=0, concat_axis=3, tiled=True)[0]


def forward_spectra(block_grouped, cos_big, sin_big, position):
    groups = block_grouped.shape[0]
    fields = block_grouped.shape[1]
    own_channels = block_grouped.shape[2]
    per_peer = block_grouped.shape[3]
    frames = groups * per_peer
    padded = 2 * frames * groups
    flat_layout = block_grouped.reshape(groups, fields * own_channels * per_peer)
    cosine, sine_table, row_index, col_index = angle_table(groups, groups, 2 * groups)
    parity = jnp.where(col_index % 2 == 0, 1.0, -1.0)
    imag_table = jnp.where(row_index == 0, parity, -sine_table)
    payload = jnp.stack([product(cosine, flat_layout), product(imag_table, flat_layout)], 1)
    payload = payload.reshape(payload.shape[0], 2, fields, own_channels, per_peer)
    received = lax.all_to_all(payload, "ctx", split_axis=0, concat_axis=4, tiled=True)
    is_zero = position == 0
    real_first = received[0, 0]
    imag_first = received[0, 1]
    real_part = jnp.stack([real_first, jnp.where(is_zero, imag_first, real_first)])
    imag_part = jnp.stack(
        [jnp.where(is_zero, 0.0, imag_first), jnp.where(is_zero, 0.0, -imag_first)]
    )
    frequencies = jnp.stack([position, jnp.where(is_zero, groups, 2 * groups - position)])
    real_part, imag_part = twiddle(real_part, imag_part, frequencies, padded, -1.0)
    rows_real = real_part.reshape(-1, frames)
    rows_imag = imag_part.reshape(-1, frames)
    out_real = product(rows_real, cos_big) + product(rows_imag, sin_big)
    out_imag = product(rows_imag, cos_big) - product(rows_real, sin_big)
    return (out_real.reshape(real_part.shape), out_imag.reshape(real_part.shape), frequencies)


def invert(real_spec, imag_spec, frequencies, cos_big, sin_big, groups, position):
    spec_shape = real_spec.shape
    fields = spec_shape[1]
    own_channels = spec_shape[2]
    frames = spec_shape[3]
    per_peer = frames // groups
    padded = 2 * frames * groups
    rows_real = real_spec.reshape(-1, frames)
    rows_imag = imag_spec.reshape(-1, frames)
    back_real = product(rows_real, cos_big) - product(rows_imag, sin_big)
    back_imag = product(rows_imag, cos_big) + product(rows_real, sin_big)
    back_real, back_imag = twiddle(
        back_real.reshape(spec_shape), back_imag.reshape(spec_shape), frequencies, padded, 1.0
    )
    is_zero = position == 0
    payload = jnp.stack([back_real[0], jnp.where(is_zero, back_real[1], back_imag[0])])[None]
    received = lax.all_to_all(payload, "ctx", split_axis=4, concat_axis=0, tiled=True)
    slot_count = received.shape[0]
    real_rows = received[:, 0].reshape(slot_count, fields * own_channels * per_peer)
    imag_rows = received[:, 1].reshape(slot_count, fields * own_channels * per_peer)
    cosine, sine_table, row_index, col_index = angle_table(groups, groups, 2 * groups)
    parity = jnp.where(row_index % 2 == 0, 1.0, -1.0)
    real_table = jnp.where(col_index == 0, 1.0, 2.0 * cosine)
    imag_table = jnp.where(col_index == 0, -parity, 2.0 * sine_table)
    result = (product(real_table, real_rows) - product(imag_table, imag_rows)) * (1.0 / padded)
    return result.reshape(groups, fields, own_channels, per_peer)


def general(inputs, proj_weight, filters, skip_gain, targets):
    frames = inputs.shape[0]
    columns = inputs.shape[1]
    channels = proj_weight.shape[2]
    groups = lax.axis_size("ctx")
    position = lax.axis_index("ctx")
    scaling = float(frames * groups) ** (-0.5)
    weight_cols = proj_weight
    projected = lax.psum_scatter(
        jnp.einsum("td,pdc->cpt", inputs, weight_cols, preferred_element_type=jnp.float32),
        "ch",
        scatter_dimension=0,
        tiled=True,
    )
    values = projected[:, 0]
    gates = projected[:, 1]
    cos_big, sin_big, row_index, col_index = angle_table(frames, frames, frames)
    skip_rows = skip_gain[:, None]
    block_grouped = to_blocks(jnp.stack([values, filters]))
    spec_real, spec_imag, frequencies = forward_spectra(block_grouped, cos_big, sin_big, position)
    conv_real, conv_imag = multiply(
        spec_real[:, 0], spec_imag[:, 0], spec_real[:, 1], spec_imag[:, 1], 1.0
    )
    conv_blocks = invert(
        conv_real[:, None], conv_imag[:, None], frequencies, cos_big, sin_big, groups, position
    )
    conv = to_frames(conv_blocks)[0] + skip_rows * values
    outputs_seq = gates * conv
    residual = outputs_seq - targets
    grad_conv = residual * gates
    grad_gate_seq = residual * conv
    grad_blocks = to_blocks(grad_conv[None])
    grad_real, grad_imag, frequencies = forward_spectra(grad_blocks, cos_big, sin_big, position)
    value_real, value_imag = multiply(
        grad_real[:, 0], grad_imag[:, 0], spec_real[:, 1], spec_imag[:, 1], -1.0
    )
    filt_real, filt_imag = multiply(
        grad_real[:, 0], grad_imag[:, 0], spec_real[:, 0], spec_imag[:, 0], -1.0
    )
    returned = invert(
        jnp.stack([value_real, filt_real], 1),
        jnp.stack([value_imag, filt_imag], 1),
        frequencies,
        cos_big,
        sin_big,
        groups,
        position,
    )
    returned_seq = to_frames(returned)
    grad_value_seq = returned_seq[0] + skip_rows * grad_conv
    grad_filter = returned_seq[1]
    grad_pair = jnp.stack([grad_value_seq, grad_gate_seq])
    inputs_wide = inputs.astype(jnp.float32)
    weight_wide = proj_weight.astype(jnp.float32)
    portion = lax.all_gather(grad_pair, "ch", axis=1, tiled=True)
    weight_cols = weight_wide
    summed_in = jnp.einsum(
        "pct,pdc->td", portion, weight_cols, precision=HIGHEST, preferred_element_type=jnp.float32
    )
    block_rows = jnp.einsum(
        "pct,td->pcd", portion, inputs_wide, precision=HIGHEST, preferred_element_type=jnp.float32
    )
    weight_rows = block_rows
    grad_inputs, weight_rows = (summed_in, weight_rows)
    grad_proj = (
        lax.psum_scatter(
            weight_rows.reshape(2 * channels, columns), "ctx", scatter_dimension=0, tiled=True
        )
        * scaling
    )
    return (outputs_seq, grad_inputs, grad_filter * scaling, grad_proj)


MESH = pl.DeviceIdType.MESH
LANES = 128
PIECES = 4
VMEM_SPEC = pl.BlockSpec(memory_space=pltpu.VMEM)


def exact_dot(left, right):
    return jnp.dot(left, right, precision=HIGHEST, preferred_element_type=jnp.float32)


def spectrum_tables(coarse, fine):
    total = 2 * coarse * fine
    half_shifted = np.arange(coarse)[:, None] + 0.5
    first = 2.0 * np.pi * half_shifted * np.arange(coarse)[None, :] / (2 * coarse)
    middle = 2.0 * np.pi * half_shifted * np.arange(fine)[None, :] / total
    last = 2.0 * np.pi * (np.outer(np.arange(fine), np.arange(fine)) % fine) / fine
    cosine, sine = np.cos(last), np.sin(last)
    return (
        np.concatenate([np.cos(first), -np.sin(first)], 0),
        np.stack([np.cos(middle), -np.sin(middle)]),
        np.block([[cosine, -sine], [sine, cosine]]),
        np.block([[cosine, sine], [-sine, cosine]]),
        np.concatenate([np.cos(first.T), -np.sin(first.T)], 1) * (2.0 / total),
    )


def project_kernel(own, x_ref, w_ref, filters_ref, targets_ref, wide_ref, narrow_ref):
    owners, groups = wide_ref.shape[0], wide_ref.shape[1]
    for p in range(2):
        rows = jnp.dot(x_ref[...], w_ref[p], preferred_element_type=jnp.float32).T
        for k in range(owners * groups):
            wide_ref[k // groups, k % groups, p * own : (p + 1) * own, :] = rows[
                k * own : (k + 1) * own, :
            ]
    for g in range(groups):
        narrow_ref[g, :own, :] = filters_ref[g * own : (g + 1) * own, :]
        narrow_ref[g, own:, :] = targets_ref[g * own : (g + 1) * own, :]


def exchange_kernel(
    groups, halves, own_wide, wide_ref, narrow_ref, wide_out, narrow_out, sent_w, got_w, sent_n, got_n, kept
):
    c, h = lax.axis_index("ctx"), lax.axis_index("ch")
    total = groups * halves
    me = h * groups + c
    barrier = pltpu.get_barrier_semaphore()
    for k in range(1, total):
        peer = lax.rem(me + k, total)
        pl.semaphore_signal(
            barrier, inc=1, device_id=(lax.rem(peer, groups), peer // groups), device_id_type=MESH
        )
    pl.semaphore_wait(barrier, total - 1)
    copies = []
    for k in range(1, total):
        peer = lax.rem(me + k, total)
        peer_c, peer_h = lax.rem(peer, groups), peer // groups
        copies.append(
            pltpu.make_async_remote_copy(
                src_ref=wide_ref.at[peer_h, peer_c] if own_wide else wide_ref.at[peer_c],
                dst_ref=wide_out.at[h, c],
                send_sem=sent_w.at[k],
                recv_sem=got_w.at[k],
                device_id=(peer_c, peer_h),
                device_id_type=MESH,
            )
        )
    for k in range(1, groups):
        peer_c = lax.rem(c + k, groups)
        copies.append(
            pltpu.make_async_remote_copy(
                src_ref=narrow_ref.at[peer_c],
                dst_ref=narrow_out.at[c],
                send_sem=sent_n.at[k],
                recv_sem=got_n.at[k],
                device_id=(peer_c, h),
                device_id_type=MESH,
            )
        )
    for copy in copies:
        copy.start()
    local_w = pltpu.make_async_copy(
        wide_ref.at[h, c] if own_wide else wide_ref.at[c], wide_out.at[h, c], kept.at[0]
    )
    local_n = pltpu.make_async_copy(narrow_ref.at[c], narrow_out.at[c], kept.at[1])
    local_w.start()
    local_n.start()
    local_w.wait()
    local_n.wait()
    for copy in copies:
        copy.wait()


def exchange(wide, narrow, halves, collective_id):
    groups = narrow.shape[0]
    block = narrow.shape[1:]
    total = groups * halves
    return pl.pallas_call(
        functools.partial(exchange_kernel, groups, halves, wide.ndim == 4),
        out_shape=(
            jax.ShapeDtypeStruct((halves, groups) + block, jnp.float32),
            jax.ShapeDtypeStruct((groups,) + block, jnp.float32),
        ),
        in_specs=[VMEM_SPEC] * 2,
        out_specs=(VMEM_SPEC,) * 2,
        scratch_shapes=[
            pltpu.SemaphoreType.DMA((total,)),
            pltpu.SemaphoreType.DMA((total,)),
            pltpu.SemaphoreType.DMA((groups,)),
            pltpu.SemaphoreType.DMA((groups,)),
            pltpu.SemaphoreType.DMA((2,)),
        ],
        compiler_params=pltpu.CompilerParams(collective_id=collective_id, has_side_effects=True),
    )(wide, narrow)


def operator_kernel(
    own, scaling, wide_ref, narrow_ref, skip_ref, t1_ref, mid_ref, t2_ref, t2i_ref, t1i_ref, pair_ref, done_ref
):
    halves, groups, _, frames = wide_ref.shape
    splits = frames // LANES
    coarse = groups * splits
    c0 = lax.axis_index("ctx") * own
    mid_real, mid_imag = mid_ref[0], mid_ref[1]

    def channels(array):
        return [array[:, c * LANES : (c + 1) * LANES] for c in range(own)]

    def gather(rows):
        return jnp.concatenate(
            [
                jnp.concatenate([row[:, s * LANES : (s + 1) * LANES] for row in rows], 1)
                for s in range(splits)
            ],
            0,
        )

    def spread(ref, base, array):
        for c in range(own):
            for s in range(splits):
                ref[:, base + c, s * LANES : (s + 1) * LANES] = array[
                    s * groups : (s + 1) * groups, c * LANES : (c + 1) * LANES
                ]

    def forward(array):
        stage = exact_dot(t1_ref[...], array)
        rows = []
        for part in channels(stage):
            real, imag = part[:coarse], part[coarse:]
            rows.append(
                jnp.concatenate(
                    [real * mid_real - imag * mid_imag, real * mid_imag + imag * mid_real], 1
                )
            )
        return exact_dot(jnp.concatenate(rows, 0), t2_ref[...])

    def backward(spectrum):
        stage = exact_dot(spectrum, t2i_ref[...])
        columns = []
        for c in range(own):
            real = stage[c * coarse : (c + 1) * coarse, :LANES]
            imag = stage[c * coarse : (c + 1) * coarse, LANES:]
            columns.append(
                jnp.concatenate(
                    [real * mid_real + imag * mid_imag, imag * mid_real - real * mid_imag], 0
                )
            )
        return exact_dot(t1i_ref[...], jnp.concatenate(columns, 1))

    def times(left, right, sign):
        left_real, left_imag = left[:, :LANES], left[:, LANES:]
        right_real, right_imag = right[:, :LANES], sign * right[:, LANES:]
        return jnp.concatenate(
            [
                left_real * right_real - left_imag * right_imag,
                left_real * right_imag + left_imag * right_real,
            ],
            1,
        )

    def summed(row):
        value = wide_ref[0, :, row, :]
        for h in range(1, halves):
            value = value + wide_ref[h, :, row, :]
        return value

    values = gather([summed(c) for c in range(own)])
    gates = gather([summed(own + c) for c in range(own)])
    filters = gather([narrow_ref[:, c, :] for c in range(own)])
    targets = gather([narrow_ref[:, own + c, :] for c in range(own)])
    skip = jnp.concatenate(
        [jnp.full((1, LANES), skip_ref[c0 + c], jnp.float32) for c in range(own)], 1
    )
    value_spec = forward(values)
    filter_spec = forward(filters)
    conv = backward(times(value_spec, filter_spec, 1.0)) + skip * values
    outputs = gates * conv
    residual = outputs - targets
    grad_conv = residual * gates
    spread(done_ref, 0, outputs)
    spread(pair_ref, own, residual * conv)
    grad_spec = forward(grad_conv)
    spread(
        pair_ref, 0, backward(times(grad_spec, filter_spec, -1.0)) + skip * grad_conv
    )
    spread(done_ref, own, backward(times(grad_spec, value_spec, -1.0)) * scaling)


def split(array):
    high = array.astype(jnp.bfloat16)
    return high, (array - high.astype(jnp.float32)).astype(jnp.bfloat16)


def gradient_kernel(
    own, wide_ref, narrow_ref, x_ref, w_ref, outputs_ref, filter_ref, grad_in_ref, partial_ref, pair_ref
):
    halves, groups, _, frames = wide_ref.shape
    channels = halves * groups * own
    for g in range(groups):
        outputs_ref[g * own : (g + 1) * own, :] = narrow_ref[g, :own, :]
        filter_ref[g * own : (g + 1) * own, :] = narrow_ref[g, own:, :]
    for p in range(2):
        for k in range(halves * groups):
            base = p * channels + k * own
            pair_ref[base : base + own, :] = wide_ref[
                k // groups, k % groups, p * own : (p + 1) * own, :
            ]
    high, low = split(pair_ref[...])
    columns = x_ref.shape[1]
    width = columns // PIECES
    for j in range(PIECES):
        cut = slice(j * width, (j + 1) * width)
        x = x_ref[:, cut]
        product_rows = jnp.dot(high, x, preferred_element_type=jnp.float32) + jnp.dot(
            low, x, preferred_element_type=jnp.float32
        )
        partial_ref[..., cut] = product_rows.reshape(partial_ref.shape[:-1] + (width,))
    flipped_high, flipped_low = split(pair_ref[...].T)
    flip = (((1,), (1,)), ((), ()))
    for j in range(PIECES):
        cut = slice(j * width, (j + 1) * width)
        w = jnp.concatenate([w_ref[0, cut, :], w_ref[1, cut, :]], 1)
        grad_in_ref[:, cut] = lax.dot_general(
            flipped_high, w, flip, preferred_element_type=jnp.float32
        ) + lax.dot_general(flipped_low, w, flip, preferred_element_type=jnp.float32)


def reduce_kernel(
    scaling, part_ref, out_ref, in1, sum1, in2, sum2, in3, s1, g1, s2, g2, s3, g3
):
    far, _, _, rows, columns = part_ref.shape
    c, h = lax.axis_index("ctx"), lax.axis_index("ch")
    core, x, z = lax.rem(c, 2), lax.rem(c // 2, 2), c // 4
    core_peer = c + 1 - 2 * core
    x_peer = c + 2 - 4 * x
    barrier = pltpu.get_barrier_semaphore()
    z_peers = [lax.rem(c + 4 * d, 4 * far) for d in range(1, far)]
    for peer in [core_peer, x_peer] + z_peers:
        pl.semaphore_signal(barrier, inc=1, device_id=(peer, h), device_id_type=MESH)
    pl.semaphore_wait(barrier, far + 1)
    width = columns // PIECES
    cuts = [pl.ds(j * width, width) for j in range(PIECES)]

    def send(source, target, send_sem, recv_sem, peer):
        copy = pltpu.make_async_remote_copy(
            src_ref=source,
            dst_ref=target,
            send_sem=send_sem,
            recv_sem=recv_sem,
            device_id=(peer, h),
            device_id_type=MESH,
        )
        copy.start()
        return copy

    first = [
        send(part_ref.at[:, :, 1 - core, :, cut], in1.at[:, :, :, cut], s1.at[j], g1.at[j], core_peer)
        for j, cut in enumerate(cuts)
    ]
    second = []
    for j, cut in enumerate(cuts):
        first[j].wait()
        sum1[:, :, :, cut] = part_ref[:, :, core, :, cut] + in1[:, :, :, cut]
        second.append(
            send(sum1.at[:, 1 - x, :, cut], in2.at[:, :, cut], s2.at[j], g2.at[j], x_peer)
        )
    third = []
    for j, cut in enumerate(cuts):
        second[j].wait()
        sum2[:, :, cut] = sum1[:, x, :, cut] + in2[:, :, cut]
        third.append(
            [
                send(
                    sum2.at[z_peers[d] // 4, :, cut],
                    in3.at[d, :, cut],
                    s3.at[j, d],
                    g3.at[j, d],
                    z_peers[d],
                )
                for d in range(far - 1)
            ]
        )
    for j, cut in enumerate(cuts):
        total = sum2[z, :, cut]
        for d in range(far - 1):
            third[j][d].wait()
            total = total + in3[d, :, cut]
        out_ref[:, cut] = total * scaling


def per_device(inputs, proj_weight, filters, skip_gain, targets):
    groups, halves = lax.axis_size("ctx"), lax.axis_size("ch")
    frames, columns = inputs.shape
    channels = proj_weight.shape[2]
    own = channels // (groups * halves)
    fits = own * groups * halves == channels and own == 4 and groups % 8 == 0
    if not fits or frames % LANES:
        return general(inputs, proj_weight, filters, skip_gain, targets)
    length = frames * groups
    scaling = float(length) ** -0.5
    splits = frames // LANES
    t1, mid, t2, t2i, t1i = spectrum_tables(length // LANES, LANES)
    order = np.arange(length // LANES).reshape(groups, splits).T.reshape(-1)
    tables = [
        jnp.asarray(table, jnp.float32) for table in (t1[:, order], mid, t2, t2i, t1i[order])
    ]
    f32 = jnp.float32
    block = (2 * own, frames)
    big = pltpu.CompilerParams(vmem_limit_bytes=60 * 1024 * 1024)
    wide, narrow = pl.pallas_call(
        functools.partial(project_kernel, own),
        out_shape=(
            jax.ShapeDtypeStruct((halves, groups) + block, f32),
            jax.ShapeDtypeStruct((groups,) + block, f32),
        ),
        in_specs=[VMEM_SPEC] * 4,
        out_specs=(VMEM_SPEC,) * 2,
        compiler_params=big,
    )(inputs, proj_weight, filters, targets)
    wide, narrow = exchange(wide, narrow, halves, 0)
    pair, done = pl.pallas_call(
        functools.partial(operator_kernel, own, scaling),
        out_shape=(jax.ShapeDtypeStruct((groups,) + block, f32),) * 2,
        in_specs=[VMEM_SPEC] * 2 + [pl.BlockSpec(memory_space=pltpu.SMEM)] + [VMEM_SPEC] * 5,
        out_specs=(VMEM_SPEC,) * 2,
        compiler_params=big,
    )(wide, narrow, skip_gain, *tables)
    wide, narrow = exchange(pair, done, halves, 1)
    rows = 2 * channels // groups
    outputs, grad_filter, grad_inputs, partial = pl.pallas_call(
        functools.partial(gradient_kernel, own),
        out_shape=(
            jax.ShapeDtypeStruct(filters.shape, f32),
            jax.ShapeDtypeStruct(filters.shape, f32),
            jax.ShapeDtypeStruct((frames, columns), f32),
            jax.ShapeDtypeStruct((groups // 4, 2, 2, rows, columns), f32),
        ),
        in_specs=[VMEM_SPEC] * 4,
        out_specs=(VMEM_SPEC,) * 4,
        scratch_shapes=[pltpu.VMEM((2 * channels, frames), f32)],
        compiler_params=big,
    )(wide, narrow, inputs, proj_weight)
    far = groups // 4
    dma = pltpu.SemaphoreType.DMA
    grad_proj = pl.pallas_call(
        functools.partial(reduce_kernel, scaling),
        out_shape=jax.ShapeDtypeStruct((rows, columns), f32),
        in_specs=[VMEM_SPEC],
        out_specs=VMEM_SPEC,
        scratch_shapes=[
            pltpu.VMEM((far, 2, rows, columns), f32),
            pltpu.VMEM((far, 2, rows, columns), f32),
            pltpu.VMEM((far, rows, columns), f32),
            pltpu.VMEM((far, rows, columns), f32),
            pltpu.VMEM((far - 1, rows, columns), f32),
            dma((PIECES,)),
            dma((PIECES,)),
            dma((PIECES,)),
            dma((PIECES,)),
            dma((PIECES, far - 1)),
            dma((PIECES, far - 1)),
        ],
        compiler_params=pltpu.CompilerParams(
            collective_id=2, has_side_effects=True, vmem_limit_bytes=60 * 1024 * 1024
        ),
    )(partial)
    return outputs, grad_inputs, grad_filter, grad_proj


def solution(mesh):
    placed = (P("ctx", "ch"), P(None, "ch", None), P("ch", "ctx"), P("ch"), P("ch", "ctx"))
    return jax.shard_map(
        per_device,
        mesh=mesh,
        in_specs=placed,
        out_specs=(P("ch", "ctx"), P("ctx", "ch"), P("ch", "ctx"), P("ctx", "ch")),
        check_vma=False,
    )
```

```python
import math

import functools

import jax
import jax.numpy as jnp
import numpy as np
from jax import lax
from jax.experimental import pallas as pl
from jax.experimental.pallas import tpu as pltpu
from jax.sharding import PartitionSpec as P

HIGHEST = lax.Precision.HIGHEST


def product(left, right):
    return jnp.dot(left, right, precision=HIGHEST, preferred_element_type=jnp.float32)


def angle_table(row_total, col_total, period):
    row_index = lax.broadcasted_iota(jnp.int32, (row_total, col_total), 0)
    col_index = lax.broadcasted_iota(jnp.int32, (row_total, col_total), 1)
    phase_index = row_index * col_index % period
    angles = 2.0 * math.pi / period * phase_index.astype(jnp.float32)
    return (jnp.cos(angles), jnp.sin(angles), row_index, col_index)


def twiddle(real_part, imag_part, frequencies, padded, direction):
    frames = real_part.shape[-1]
    offsets = lax.broadcasted_iota(jnp.int32, (2, frames), 1)
    phase_index = frequencies[:, None] * offsets % padded
    angles = direction * 2.0 * math.pi / padded * phase_index.astype(jnp.float32)
    cosine = jnp.cos(angles)[:, None, None, :]
    sine_table = jnp.sin(angles)[:, None, None, :]
    return (
        real_part * cosine - imag_part * sine_table,
        real_part * sine_table + imag_part * cosine,
    )


def multiply(left_real, left_imag, right_real, right_imag, conj_sign):
    right_imag = conj_sign * right_imag
    return (
        left_real * right_real - left_imag * right_imag,
        left_real * right_imag + left_imag * right_real,
    )


def to_blocks(fields_seq):
    return lax.all_to_all(fields_seq[None], "ctx", split_axis=3, concat_axis=0, tiled=True)


def to_frames(block_grouped):
    return lax.all_to_all(block_grouped, "ctx", split_axis=0, concat_axis=3, tiled=True)[0]


def forward_spectra(block_grouped, cos_big, sin_big, position):
    groups = block_grouped.shape[0]
    fields = block_grouped.shape[1]
    own_channels = block_grouped.shape[2]
    per_peer = block_grouped.shape[3]
    frames = groups * per_peer
    padded = 2 * frames * groups
    flat_layout = block_grouped.reshape(groups, fields * own_channels * per_peer)
    cosine, sine_table, row_index, col_index = angle_table(groups, groups, 2 * groups)
    parity = jnp.where(col_index % 2 == 0, 1.0, -1.0)
    imag_table = jnp.where(row_index == 0, parity, -sine_table)
    payload = jnp.stack([product(cosine, flat_layout), product(imag_table, flat_layout)], 1)
    payload = payload.reshape(payload.shape[0], 2, fields, own_channels, per_peer)
    received = lax.all_to_all(payload, "ctx", split_axis=0, concat_axis=4, tiled=True)
    is_zero = position == 0
    real_first = received[0, 0]
    imag_first = received[0, 1]
    real_part = jnp.stack([real_first, jnp.where(is_zero, imag_first, real_first)])
    imag_part = jnp.stack(
        [jnp.where(is_zero, 0.0, imag_first), jnp.where(is_zero, 0.0, -imag_first)]
    )
    frequencies = jnp.stack([position, jnp.where(is_zero, groups, 2 * groups - position)])
    real_part, imag_part = twiddle(real_part, imag_part, frequencies, padded, -1.0)
    rows_real = real_part.reshape(-1, frames)
    rows_imag = imag_part.reshape(-1, frames)
    out_real = product(rows_real, cos_big) + product(rows_imag, sin_big)
    out_imag = product(rows_imag, cos_big) - product(rows_real, sin_big)
    return (out_real.reshape(real_part.shape), out_imag.reshape(real_part.shape), frequencies)


def invert(real_spec, imag_spec, frequencies, cos_big, sin_big, groups, position):
    spec_shape = real_spec.shape
    fields = spec_shape[1]
    own_channels = spec_shape[2]
    frames = spec_shape[3]
    per_peer = frames // groups
    padded = 2 * frames * groups
    rows_real = real_spec.reshape(-1, frames)
    rows_imag = imag_spec.reshape(-1, frames)
    back_real = product(rows_real, cos_big) - product(rows_imag, sin_big)
    back_imag = product(rows_imag, cos_big) + product(rows_real, sin_big)
    back_real, back_imag = twiddle(
        back_real.reshape(spec_shape), back_imag.reshape(spec_shape), frequencies, padded, 1.0
    )
    is_zero = position == 0
    payload = jnp.stack([back_real[0], jnp.where(is_zero, back_real[1], back_imag[0])])[None]
    received = lax.all_to_all(payload, "ctx", split_axis=4, concat_axis=0, tiled=True)
    slot_count = received.shape[0]
    real_rows = received[:, 0].reshape(slot_count, fields * own_channels * per_peer)
    imag_rows = received[:, 1].reshape(slot_count, fields * own_channels * per_peer)
    cosine, sine_table, row_index, col_index = angle_table(groups, groups, 2 * groups)
    parity = jnp.where(row_index % 2 == 0, 1.0, -1.0)
    real_table = jnp.where(col_index == 0, 1.0, 2.0 * cosine)
    imag_table = jnp.where(col_index == 0, -parity, 2.0 * sine_table)
    result = (product(real_table, real_rows) - product(imag_table, imag_rows)) * (1.0 / padded)
    return result.reshape(groups, fields, own_channels, per_peer)


def general(inputs, proj_weight, filters, skip_gain, targets):
    frames = inputs.shape[0]
    columns = inputs.shape[1]
    channels = proj_weight.shape[2]
    groups = lax.axis_size("ctx")
    position = lax.axis_index("ctx")
    scaling = float(frames * groups) ** (-0.5)
    weight_cols = proj_weight
    projected = lax.psum_scatter(
        jnp.einsum("td,pdc->cpt", inputs, weight_cols, preferred_element_type=jnp.float32),
        "ch",
        scatter_dimension=0,
        tiled=True,
    )
    values = projected[:, 0]
    gates = projected[:, 1]
    cos_big, sin_big, row_index, col_index = angle_table(frames, frames, frames)
    skip_rows = skip_gain[:, None]
    block_grouped = to_blocks(jnp.stack([values, filters]))
    spec_real, spec_imag, frequencies = forward_spectra(block_grouped, cos_big, sin_big, position)
    conv_real, conv_imag = multiply(
        spec_real[:, 0], spec_imag[:, 0], spec_real[:, 1], spec_imag[:, 1], 1.0
    )
    conv_blocks = invert(
        conv_real[:, None], conv_imag[:, None], frequencies, cos_big, sin_big, groups, position
    )
    conv = to_frames(conv_blocks)[0] + skip_rows * values
    outputs_seq = gates * conv
    residual = outputs_seq - targets
    grad_conv = residual * gates
    grad_gate_seq = residual * conv
    grad_blocks = to_blocks(grad_conv[None])
    grad_real, grad_imag, frequencies = forward_spectra(grad_blocks, cos_big, sin_big, position)
    value_real, value_imag = multiply(
        grad_real[:, 0], grad_imag[:, 0], spec_real[:, 1], spec_imag[:, 1], -1.0
    )
    filt_real, filt_imag = multiply(
        grad_real[:, 0], grad_imag[:, 0], spec_real[:, 0], spec_imag[:, 0], -1.0
    )
    returned = invert(
        jnp.stack([value_real, filt_real], 1),
        jnp.stack([value_imag, filt_imag], 1),
        frequencies,
        cos_big,
        sin_big,
        groups,
        position,
    )
    returned_seq = to_frames(returned)
    grad_value_seq = returned_seq[0] + skip_rows * grad_conv
    grad_filter = returned_seq[1]
    grad_pair = jnp.stack([grad_value_seq, grad_gate_seq])
    inputs_wide = inputs.astype(jnp.float32)
    weight_wide = proj_weight.astype(jnp.float32)
    portion = lax.all_gather(grad_pair, "ch", axis=1, tiled=True)
    weight_cols = weight_wide
    summed_in = jnp.einsum(
        "pct,pdc->td", portion, weight_cols, precision=HIGHEST, preferred_element_type=jnp.float32
    )
    block_rows = jnp.einsum(
        "pct,td->pcd", portion, inputs_wide, precision=HIGHEST, preferred_element_type=jnp.float32
    )
    weight_rows = block_rows
    grad_inputs, weight_rows = (summed_in, weight_rows)
    grad_proj = (
        lax.psum_scatter(
            weight_rows.reshape(2 * channels, columns), "ctx", scatter_dimension=0, tiled=True
        )
        * scaling
    )
    return (outputs_seq, grad_inputs, grad_filter * scaling, grad_proj)


MESH = pl.DeviceIdType.MESH
LANES = 128
PIECES = 8
BITES = 2
VMEM_SPEC = pl.BlockSpec(memory_space=pltpu.VMEM)


def exact_dot(left, right):
    return jnp.dot(left, right, precision=HIGHEST, preferred_element_type=jnp.float32)


def spectrum_tables(coarse, fine):
    total = 2 * coarse * fine
    half_shifted = np.arange(coarse)[:, None] + 0.5
    first = 2.0 * np.pi * half_shifted * np.arange(coarse)[None, :] / (2 * coarse)
    middle = 2.0 * np.pi * half_shifted * np.arange(fine)[None, :] / total
    last = 2.0 * np.pi * (np.outer(np.arange(fine), np.arange(fine)) % fine) / fine
    cosine, sine = np.cos(last), np.sin(last)
    return (
        np.concatenate([np.cos(first), -np.sin(first)], 0),
        np.stack([np.cos(middle), -np.sin(middle)]),
        np.block([[cosine, -sine], [sine, cosine]]),
        np.block([[cosine, sine], [-sine, cosine]]),
        np.concatenate([np.cos(first.T), -np.sin(first.T)], 1) * (2.0 / total),
    )


def split(array):
    high = array.astype(jnp.bfloat16)
    return high, (array - high.astype(jnp.float32)).astype(jnp.bfloat16)


def main_kernel(
    own, scaling,
    x_ref, w_ref, filters_ref, targets_ref, skip_ref, t1_ref, mid_ref, t2_ref, t2i_ref, t1i_ref,
    outputs_ref, filter_ref, pair_ref, proj_ref,
    fixed, fixed_in, halves_out, halves_in, fields, fields_in, back_out, back_in,
    part, in1, sum1, in2, sum2, in3,
    fixed_s, fixed_g, half_s, half_g, field_s, field_g, back_s, back_g, relay_s, relay_g,
    s1, g1, s2, g2, s3, g3,
):
    groups, frames = fixed.shape[0], fixed.shape[2]
    columns = x_ref.shape[1]
    splits = frames // LANES
    coarse = groups * splits
    bite = frames // BITES
    channels = 2 * groups * own
    far = groups // 4
    c, h = lax.axis_index("ctx"), lax.axis_index("ch")
    core, x_side, z = lax.rem(c, 2), lax.rem(c // 2, 2), c // 4
    core_peer = c + 1 - 2 * core
    x_peer = c + 2 - 4 * x_side
    z_peers = [lax.rem(c + 4 * d, groups) for d in range(1, far)]
    peers = [lax.rem(c + k, groups) for k in range(1, groups)]
    sources = [lax.rem(c + groups - k, groups) for k in range(1, groups)]
    sent = []

    def send(source, target, send_sem, recv_sem, peer_c, peer_h):
        copy = pltpu.make_async_remote_copy(
            src_ref=source,
            dst_ref=target,
            send_sem=send_sem,
            recv_sem=recv_sem,
            device_id=(peer_c, peer_h),
            device_id_type=MESH,
        )
        copy.start()
        sent.append(copy)
        return copy

    barrier = pltpu.get_barrier_semaphore()
    for peer in peers:
        pl.semaphore_signal(barrier, inc=1, device_id=(peer, h), device_id_type=MESH)
    pl.semaphore_signal(barrier, inc=1, device_id=(c, 1 - h), device_id_type=MESH)

    for g in range(groups):
        fixed[g, :own, :] = filters_ref[g * own : (g + 1) * own, :]
        fixed[g, own:, :] = targets_ref[g * own : (g + 1) * own, :]

    def project(q):
        for p in range(2):
            rows = jnp.dot(
                x_ref[q * bite : (q + 1) * bite, :], w_ref[p], preferred_element_type=jnp.float32
            ).T
            for k in range(2 * groups):
                halves_out[q, k // groups, k % groups, p * own : (p + 1) * own, :] = rows[
                    k * own : (k + 1) * own, :
                ]

    project(0)
    pl.semaphore_wait(barrier, groups)
    half_copies, fixed_copies, field_copies = [], [], []

    def send_half(q):
        half_copies.append(
            send(halves_out.at[q, 1 - h], halves_in.at[q], half_s.at[q], half_g.at[q], c, 1 - h)
        )

    send_half(0)
    for k, peer in enumerate(peers):
        fixed_copies.append(
            send(fixed.at[peer], fixed_in.at[c], fixed_s.at[k], fixed_g.at[k], peer, h)
        )
    fixed_in[c] = fixed[c]
    for q in range(1, BITES):
        project(q)
        send_half(q)
    for q in range(BITES):
        half_copies[q].wait_recv()
        fields[q] = halves_out[q, h] + halves_in[q]
        for k, peer in enumerate(peers):
            field_copies.append(
                send(fields.at[q, peer], fields_in.at[q, c], field_s.at[q, k], field_g.at[q, k], peer, h)
            )
        fields_in[q, c] = fields[q, c]

    mid_real, mid_imag = mid_ref[0], mid_ref[1]

    def gather(rows):
        return jnp.concatenate(
            [
                jnp.concatenate([row[:, s * LANES : (s + 1) * LANES] for row in rows], 1)
                for s in range(splits)
            ],
            0,
        )

    def spread(field, array):
        for i in range(own):
            for s in range(splits):
                back_out[field, :, i, s * LANES : (s + 1) * LANES] = array[
                    s * groups : (s + 1) * groups, i * LANES : (i + 1) * LANES
                ]

    def forward(array):
        stage = exact_dot(t1_ref[...], array)
        rows = []
        for i in range(own):
            real = stage[:coarse, i * LANES : (i + 1) * LANES]
            imag = stage[coarse:, i * LANES : (i + 1) * LANES]
            rows.append(
                jnp.concatenate(
                    [real * mid_real - imag * mid_imag, real * mid_imag + imag * mid_real], 1
                )
            )
        return exact_dot(jnp.concatenate(rows, 0), t2_ref[...])

    def backward(spectrum):
        stage = exact_dot(spectrum, t2i_ref[...])
        blocks = []
        for i in range(own):
            real = stage[i * coarse : (i + 1) * coarse, :LANES]
            imag = stage[i * coarse : (i + 1) * coarse, LANES:]
            blocks.append(
                jnp.concatenate(
                    [real * mid_real + imag * mid_imag, imag * mid_real - real * mid_imag], 0
                )
            )
        return exact_dot(t1i_ref[...], jnp.concatenate(blocks, 1))

    def times(left, right, sign):
        left_real, left_imag = left[:, :LANES], left[:, LANES:]
        right_real, right_imag = right[:, :LANES], sign * right[:, LANES:]
        return jnp.concatenate(
            [
                left_real * right_real - left_imag * right_imag,
                left_real * right_imag + left_imag * right_real,
            ],
            1,
        )

    def field(row):
        return jnp.concatenate([fields_in[q, :, row, :] for q in range(BITES)], 1)

    for copy in fixed_copies:
        copy.wait_recv()
    filters = gather([fixed_in[:, i, :] for i in range(own)])
    targets = gather([fixed_in[:, own + i, :] for i in range(own)])
    skip = jnp.concatenate(
        [jnp.full((1, LANES), skip_ref[c * own + i], jnp.float32) for i in range(own)], 1
    )
    filter_spec = forward(filters)
    for copy in field_copies:
        copy.wait_recv()
    values = gather([field(i) for i in range(own)])
    gates = gather([field(own + i) for i in range(own)])
    value_spec = forward(values)
    conv = backward(times(value_spec, filter_spec, 1.0)) + skip * values
    outputs = gates * conv
    residual = outputs - targets
    grad_conv = residual * gates

    def send_back(f, target):
        return [
            send(back_out.at[f, peer], target, back_s.at[f, k], back_g.at[f, k], peer, h)
            for k, peer in enumerate(peers)
        ]

    def relay(f, copies):
        flows = [send(back_in.at[f, h, c], back_in.at[f, h, c], relay_s.at[f, 0], relay_g.at[f, 0], c, 1 - h)]
        for k, source in enumerate(sources):
            copies[k].wait_recv()
            place = back_in.at[f, h, source]
            flows.append(send(place, place, relay_s.at[f, k + 1], relay_g.at[f, k + 1], c, 1 - h))
        return flows

    spread(1, residual * conv)
    back_in[1, h, c] = back_out[1, c]
    gate_copies = send_back(1, back_in.at[1, h, c])
    spread(2, outputs)
    grad_spec = forward(grad_conv)
    spread(0, backward(times(grad_spec, filter_spec, -1.0)) + skip * grad_conv)
    back_in[0, h, c] = back_out[0, c]
    value_copies = send_back(0, back_in.at[0, h, c])
    late = send_back(2, outputs_ref.at[c])
    flows = relay(1, gate_copies)
    spread(3, backward(times(grad_spec, value_spec, -1.0)) * scaling)
    flows += relay(0, value_copies)
    late += send_back(3, filter_ref.at[c])
    outputs_ref[c] = back_out[2, c]
    filter_ref[c] = back_out[3, c]
    for copy in flows:
        copy.wait_recv()

    for p in range(2):
        for k in range(2 * groups):
            base = p * channels + k * own
            pair_ref[base : base + own, :] = back_in[p, k // groups, k % groups]
    high, low = split(pair_ref[...])
    width = columns // PIECES
    cuts = [pl.ds(j * width, width) for j in range(PIECES)]
    first, second, third = [], [], []
    for j, cut in enumerate(cuts):
        piece = x_ref[:, cut]
        product_rows = jnp.dot(high, piece, preferred_element_type=jnp.float32) + jnp.dot(
            low, piece, preferred_element_type=jnp.float32
        )
        part[..., cut] = product_rows.reshape(part.shape[:-1] + (width,))
        first.append(
            send(part.at[:, :, 1 - core, :, cut], in1.at[:, :, :, cut], s1.at[j], g1.at[j], core_peer, h)
        )
    for j, cut in enumerate(cuts):
        first[j].wait_recv()
        sum1[:, :, :, cut] = part[:, :, core, :, cut] + in1[:, :, :, cut]
        second.append(
            send(sum1.at[:, 1 - x_side, :, cut], in2.at[:, :, cut], s2.at[j], g2.at[j], x_peer, h)
        )
    for j, cut in enumerate(cuts):
        second[j].wait_recv()
        sum2[:, :, cut] = sum1[:, x_side, :, cut] + in2[:, :, cut]
        third.append(
            [
                send(
                    sum2.at[peer // 4, :, cut], in3.at[d, :, cut], s3.at[j, d], g3.at[j, d], peer, h
                )
                for d, peer in enumerate(z_peers)
            ]
        )
    for j, cut in enumerate(cuts):
        total = sum2[z, :, cut]
        for d in range(far - 1):
            third[j][d].wait_recv()
            total = total + in3[d, :, cut]
        proj_ref[:, cut] = total * scaling
    for copy in late:
        copy.wait_recv()
    for copy in sent:
        copy.wait_send()


def final_kernel(
    pair_ref, w_ref, outs_ref, filt_ref, proj_ref, grad_ref, outputs_ref, filter_ref, grad_proj_ref, high, low
):
    groups, own, _ = outs_ref.shape

    @pl.when(pl.program_id(0) == 0)
    def _():
        high[...], low[...] = split(pair_ref[...].T)
        grad_proj_ref[...] = proj_ref[...]
        for g in range(groups):
            outputs_ref[g * own : (g + 1) * own, :] = outs_ref[g]
            filter_ref[g * own : (g + 1) * own, :] = filt_ref[g]

    w = jnp.concatenate([w_ref[0], w_ref[1]], 1)
    flip = (((1,), (1,)), ((), ()))
    grad_ref[...] = lax.dot_general(
        high[...], w, flip, preferred_element_type=jnp.float32
    ) + lax.dot_general(low[...], w, flip, preferred_element_type=jnp.float32)


def per_device(inputs, proj_weight, filters, skip_gain, targets):
    groups, halves = lax.axis_size("ctx"), lax.axis_size("ch")
    frames, columns = inputs.shape
    channels = proj_weight.shape[2]
    own = channels // (groups * halves)
    fits = own * groups * halves == channels and own == 4 and groups % 8 == 0 and halves == 2
    if not fits or frames % (LANES * BITES) or columns % (LANES * PIECES):
        return general(inputs, proj_weight, filters, skip_gain, targets)
    length = frames * groups
    scaling = float(length) ** -0.5
    splits = frames // LANES
    t1, mid, t2, t2i, t1i = spectrum_tables(length // LANES, LANES)
    order = np.arange(length // LANES).reshape(groups, splits).T.reshape(-1)
    f32 = jnp.float32
    tables = [jnp.asarray(table, f32) for table in (t1[:, order], mid, t2, t2i, t1i[order])]
    rows = 2 * channels // groups
    far = groups // 4
    vmem, dma = pltpu.VMEM, pltpu.SemaphoreType.DMA
    bite = frames // BITES
    blocks = jax.ShapeDtypeStruct((groups, own, frames), f32)
    outs, filt, pair, proj = pl.pallas_call(
        functools.partial(main_kernel, own, scaling),
        out_shape=(
            blocks,
            blocks,
            jax.ShapeDtypeStruct((2 * channels, frames), f32),
            jax.ShapeDtypeStruct((rows, columns), f32),
        ),
        in_specs=[VMEM_SPEC] * 4 + [pl.BlockSpec(memory_space=pltpu.SMEM)] + [VMEM_SPEC] * 5,
        out_specs=(VMEM_SPEC,) * 4,
        scratch_shapes=[
            vmem((groups, 2 * own, frames), f32),
            vmem((groups, 2 * own, frames), f32),
            vmem((BITES, 2, groups, 2 * own, bite), f32),
            vmem((BITES, groups, 2 * own, bite), f32),
            vmem((BITES, groups, 2 * own, bite), f32),
            vmem((BITES, groups, 2 * own, bite), f32),
            vmem((4, groups, own, frames), f32),
            vmem((2, 2, groups, own, frames), f32),
            vmem((far, 2, 2, rows, columns), f32),
            vmem((far, 2, rows, columns), f32),
            vmem((far, 2, rows, columns), f32),
            vmem((far, rows, columns), f32),
            vmem((far, rows, columns), f32),
            vmem((far - 1, rows, columns), f32),
            dma((groups - 1,)),
            dma((groups - 1,)),
            dma((BITES,)),
            dma((BITES,)),
            dma((BITES, groups - 1)),
            dma((BITES, groups - 1)),
            dma((4, groups - 1)),
            dma((4, groups - 1)),
            dma((2, groups)),
            dma((2, groups)),
            dma((PIECES,)),
            dma((PIECES,)),
            dma((PIECES,)),
            dma((PIECES,)),
            dma((PIECES, far - 1)),
            dma((PIECES, far - 1)),
        ],
        compiler_params=pltpu.CompilerParams(
            collective_id=0, has_side_effects=True, vmem_limit_bytes=60 * 1024 * 1024
        ),
    )(inputs, proj_weight, filters, targets, skip_gain, *tables)

    def whole(*shape):
        return pl.BlockSpec(shape, lambda j: (0,) * len(shape))

    width = columns // 4
    grad_inputs, outputs, grad_filter, grad_proj = pl.pallas_call(
        final_kernel,
        grid=(4,),
        out_shape=(
            jax.ShapeDtypeStruct((frames, columns), f32),
            jax.ShapeDtypeStruct(filters.shape, f32),
            jax.ShapeDtypeStruct(filters.shape, f32),
            jax.ShapeDtypeStruct((rows, columns), f32),
        ),
        in_specs=[
            whole(2 * channels, frames),
            pl.BlockSpec((2, width, channels), lambda j: (0, j, 0)),
            whole(groups, own, frames),
            whole(groups, own, frames),
            whole(rows, columns),
        ],
        out_specs=(
            pl.BlockSpec((frames, width), lambda j: (0, j)),
            whole(*filters.shape),
            whole(*filters.shape),
            whole(rows, columns),
        ),
        scratch_shapes=[vmem((frames, 2 * channels), jnp.bfloat16)] * 2,
    )(pair, proj_weight, outs, filt, proj)
    return outputs, grad_inputs, grad_filter, grad_proj


def solution(mesh):
    placed = (P("ctx", "ch"), P(None, "ch", None), P("ch", "ctx"), P("ch"), P("ch", "ctx"))
    return jax.shard_map(
        per_device,
        mesh=mesh,
        in_specs=placed,
        out_specs=(P("ch", "ctx"), P("ctx", "ch"), P("ch", "ctx"), P("ctx", "ch")),
        check_vma=False,
    )
```

```python
import math

import functools

import jax
import jax.numpy as jnp
import numpy as np
from jax import lax
from jax.experimental import pallas as pl
from jax.experimental.pallas import tpu as pltpu
from jax.sharding import PartitionSpec as P

HIGHEST = lax.Precision.HIGHEST


def product(left, right):
    return jnp.dot(left, right, precision=HIGHEST, preferred_element_type=jnp.float32)


def angle_table(row_total, col_total, period):
    row_index = lax.broadcasted_iota(jnp.int32, (row_total, col_total), 0)
    col_index = lax.broadcasted_iota(jnp.int32, (row_total, col_total), 1)
    phase_index = row_index * col_index % period
    angles = 2.0 * math.pi / period * phase_index.astype(jnp.float32)
    return (jnp.cos(angles), jnp.sin(angles), row_index, col_index)


def twiddle(real_part, imag_part, frequencies, padded, direction):
    frames = real_part.shape[-1]
    offsets = lax.broadcasted_iota(jnp.int32, (2, frames), 1)
    phase_index = frequencies[:, None] * offsets % padded
    angles = direction * 2.0 * math.pi / padded * phase_index.astype(jnp.float32)
    cosine = jnp.cos(angles)[:, None, None, :]
    sine_table = jnp.sin(angles)[:, None, None, :]
    return (
        real_part * cosine - imag_part * sine_table,
        real_part * sine_table + imag_part * cosine,
    )


def multiply(left_real, left_imag, right_real, right_imag, conj_sign):
    right_imag = conj_sign * right_imag
    return (
        left_real * right_real - left_imag * right_imag,
        left_real * right_imag + left_imag * right_real,
    )


def to_blocks(fields_seq):
    return lax.all_to_all(fields_seq[None], "ctx", split_axis=3, concat_axis=0, tiled=True)


def to_frames(block_grouped):
    return lax.all_to_all(block_grouped, "ctx", split_axis=0, concat_axis=3, tiled=True)[0]


def forward_spectra(block_grouped, cos_big, sin_big, position):
    groups = block_grouped.shape[0]
    fields = block_grouped.shape[1]
    own_channels = block_grouped.shape[2]
    per_peer = block_grouped.shape[3]
    frames = groups * per_peer
    padded = 2 * frames * groups
    flat_layout = block_grouped.reshape(groups, fields * own_channels * per_peer)
    cosine, sine_table, row_index, col_index = angle_table(groups, groups, 2 * groups)
    parity = jnp.where(col_index % 2 == 0, 1.0, -1.0)
    imag_table = jnp.where(row_index == 0, parity, -sine_table)
    payload = jnp.stack([product(cosine, flat_layout), product(imag_table, flat_layout)], 1)
    payload = payload.reshape(payload.shape[0], 2, fields, own_channels, per_peer)
    received = lax.all_to_all(payload, "ctx", split_axis=0, concat_axis=4, tiled=True)
    is_zero = position == 0
    real_first = received[0, 0]
    imag_first = received[0, 1]
    real_part = jnp.stack([real_first, jnp.where(is_zero, imag_first, real_first)])
    imag_part = jnp.stack(
        [jnp.where(is_zero, 0.0, imag_first), jnp.where(is_zero, 0.0, -imag_first)]
    )
    frequencies = jnp.stack([position, jnp.where(is_zero, groups, 2 * groups - position)])
    real_part, imag_part = twiddle(real_part, imag_part, frequencies, padded, -1.0)
    rows_real = real_part.reshape(-1, frames)
    rows_imag = imag_part.reshape(-1, frames)
    out_real = product(rows_real, cos_big) + product(rows_imag, sin_big)
    out_imag = product(rows_imag, cos_big) - product(rows_real, sin_big)
    return (out_real.reshape(real_part.shape), out_imag.reshape(real_part.shape), frequencies)


def invert(real_spec, imag_spec, frequencies, cos_big, sin_big, groups, position):
    spec_shape = real_spec.shape
    fields = spec_shape[1]
    own_channels = spec_shape[2]
    frames = spec_shape[3]
    per_peer = frames // groups
    padded = 2 * frames * groups
    rows_real = real_spec.reshape(-1, frames)
    rows_imag = imag_spec.reshape(-1, frames)
    back_real = product(rows_real, cos_big) - product(rows_imag, sin_big)
    back_imag = product(rows_imag, cos_big) + product(rows_real, sin_big)
    back_real, back_imag = twiddle(
        back_real.reshape(spec_shape), back_imag.reshape(spec_shape), frequencies, padded, 1.0
    )
    is_zero = position == 0
    payload = jnp.stack([back_real[0], jnp.where(is_zero, back_real[1], back_imag[0])])[None]
    received = lax.all_to_all(payload, "ctx", split_axis=4, concat_axis=0, tiled=True)
    slot_count = received.shape[0]
    real_rows = received[:, 0].reshape(slot_count, fields * own_channels * per_peer)
    imag_rows = received[:, 1].reshape(slot_count, fields * own_channels * per_peer)
    cosine, sine_table, row_index, col_index = angle_table(groups, groups, 2 * groups)
    parity = jnp.where(row_index % 2 == 0, 1.0, -1.0)
    real_table = jnp.where(col_index == 0, 1.0, 2.0 * cosine)
    imag_table = jnp.where(col_index == 0, -parity, 2.0 * sine_table)
    result = (product(real_table, real_rows) - product(imag_table, imag_rows)) * (1.0 / padded)
    return result.reshape(groups, fields, own_channels, per_peer)


def general(inputs, proj_weight, filters, skip_gain, targets):
    frames = inputs.shape[0]
    columns = inputs.shape[1]
    channels = proj_weight.shape[2]
    groups = lax.axis_size("ctx")
    position = lax.axis_index("ctx")
    scaling = float(frames * groups) ** (-0.5)
    weight_cols = proj_weight
    projected = lax.psum_scatter(
        jnp.einsum("td,pdc->cpt", inputs, weight_cols, preferred_element_type=jnp.float32),
        "ch",
        scatter_dimension=0,
        tiled=True,
    )
    values = projected[:, 0]
    gates = projected[:, 1]
    cos_big, sin_big, row_index, col_index = angle_table(frames, frames, frames)
    skip_rows = skip_gain[:, None]
    block_grouped = to_blocks(jnp.stack([values, filters]))
    spec_real, spec_imag, frequencies = forward_spectra(block_grouped, cos_big, sin_big, position)
    conv_real, conv_imag = multiply(
        spec_real[:, 0], spec_imag[:, 0], spec_real[:, 1], spec_imag[:, 1], 1.0
    )
    conv_blocks = invert(
        conv_real[:, None], conv_imag[:, None], frequencies, cos_big, sin_big, groups, position
    )
    conv = to_frames(conv_blocks)[0] + skip_rows * values
    outputs_seq = gates * conv
    residual = outputs_seq - targets
    grad_conv = residual * gates
    grad_gate_seq = residual * conv
    grad_blocks = to_blocks(grad_conv[None])
    grad_real, grad_imag, frequencies = forward_spectra(grad_blocks, cos_big, sin_big, position)
    value_real, value_imag = multiply(
        grad_real[:, 0], grad_imag[:, 0], spec_real[:, 1], spec_imag[:, 1], -1.0
    )
    filt_real, filt_imag = multiply(
        grad_real[:, 0], grad_imag[:, 0], spec_real[:, 0], spec_imag[:, 0], -1.0
    )
    returned = invert(
        jnp.stack([value_real, filt_real], 1),
        jnp.stack([value_imag, filt_imag], 1),
        frequencies,
        cos_big,
        sin_big,
        groups,
        position,
    )
    returned_seq = to_frames(returned)
    grad_value_seq = returned_seq[0] + skip_rows * grad_conv
    grad_filter = returned_seq[1]
    grad_pair = jnp.stack([grad_value_seq, grad_gate_seq])
    inputs_wide = inputs.astype(jnp.float32)
    weight_wide = proj_weight.astype(jnp.float32)
    portion = lax.all_gather(grad_pair, "ch", axis=1, tiled=True)
    weight_cols = weight_wide
    summed_in = jnp.einsum(
        "pct,pdc->td", portion, weight_cols, precision=HIGHEST, preferred_element_type=jnp.float32
    )
    block_rows = jnp.einsum(
        "pct,td->pcd", portion, inputs_wide, precision=HIGHEST, preferred_element_type=jnp.float32
    )
    weight_rows = block_rows
    grad_inputs, weight_rows = (summed_in, weight_rows)
    grad_proj = (
        lax.psum_scatter(
            weight_rows.reshape(2 * channels, columns), "ctx", scatter_dimension=0, tiled=True
        )
        * scaling
    )
    return (outputs_seq, grad_inputs, grad_filter * scaling, grad_proj)


MESH = pl.DeviceIdType.MESH
LANES = 128
PIECES = 4
BITES = 2
VMEM_SPEC = pl.BlockSpec(memory_space=pltpu.VMEM)


def spectrum_tables(coarse, fine):
    total = 2 * coarse * fine
    half_shifted = np.arange(coarse)[:, None] + 0.5
    first = 2.0 * np.pi * half_shifted * np.arange(coarse)[None, :] / (2 * coarse)
    middle = 2.0 * np.pi * half_shifted * np.arange(fine)[None, :] / total
    last = 2.0 * np.pi * (np.outer(np.arange(fine), np.arange(fine)) % fine) / fine
    cosine, sine = np.cos(last), np.sin(last)
    return (
        np.concatenate([np.cos(first), -np.sin(first)], 0),
        np.stack([np.cos(middle), -np.sin(middle)]),
        np.block([[cosine, -sine], [sine, cosine]]),
        np.block([[cosine, sine], [-sine, cosine]]),
        np.concatenate([np.cos(first.T), -np.sin(first.T)], 1) * (2.0 / total),
    )


def split(array):
    high = array.astype(jnp.bfloat16)
    return high, (array - high.astype(jnp.float32)).astype(jnp.bfloat16)


def left_table(table_ref, array):
    high, low = split(array)
    return (
        jnp.dot(table_ref[0], high, preferred_element_type=jnp.float32)
        + jnp.dot(table_ref[0], low, preferred_element_type=jnp.float32)
        + jnp.dot(table_ref[1], high, preferred_element_type=jnp.float32)
    )


def right_table(array, table_ref):
    high, low = split(array)
    return (
        jnp.dot(high, table_ref[0], preferred_element_type=jnp.float32)
        + jnp.dot(low, table_ref[0], preferred_element_type=jnp.float32)
        + jnp.dot(high, table_ref[1], preferred_element_type=jnp.float32)
    )


def halves_of(table):
    high = np.asarray(table, jnp.bfloat16)
    low = np.asarray(table - np.asarray(high, np.float64), jnp.bfloat16)
    return jnp.asarray(np.stack([high, low]))


def main_kernel(
    own, scaling,
    x_ref, w_ref, filters_ref, targets_ref, skip_ref, t1_ref, mid_ref, t2_ref, t2i_ref, t1i_ref,
    outputs_ref, filter_ref, high_ref, low_ref, proj_ref,
    fixed, fixed_in, halves_out, halves_in, fields, fields_in, back_out, back_in,
    pair, part, in1, sum1, in2, sum2, in3,
    fixed_s, fixed_g, half_s, half_g, field_s, field_g, back_s, back_g, relay_s, relay_g,
    s1, g1, s2, g2, s3, g3,
):
    groups, frames = fixed.shape[1], fixed.shape[3]
    columns = x_ref.shape[1]
    splits = frames // LANES
    coarse = groups * splits
    bite = frames // BITES
    far = groups // 4
    c, h = lax.axis_index("ctx"), lax.axis_index("ch")
    core, x_side, z = lax.rem(c, 2), lax.rem(c // 2, 2), c // 4
    core_peer = c + 1 - 2 * core
    x_peer = c + 2 - 4 * x_side
    z_peers = [lax.rem(c + 4 * d, groups) for d in range(1, far)]
    peers = [lax.rem(c + k, groups) for k in range(1, groups)]
    sources = [lax.rem(c + groups - k, groups) for k in range(1, groups)]
    sent = []

    def send(source, target, send_sem, recv_sem, peer_c, peer_h):
        copy = pltpu.make_async_remote_copy(
            src_ref=source,
            dst_ref=target,
            send_sem=send_sem,
            recv_sem=recv_sem,
            device_id=(peer_c, peer_h),
            device_id_type=MESH,
        )
        copy.start()
        sent.append(copy)
        return copy

    barrier = pltpu.get_barrier_semaphore()
    for peer in peers:
        pl.semaphore_signal(barrier, inc=1, device_id=(peer, h), device_id_type=MESH)
    pl.semaphore_signal(barrier, inc=1, device_id=(c, 1 - h), device_id_type=MESH)

    for g in range(groups):
        fixed[0, g] = filters_ref[g * own : (g + 1) * own, :]
        fixed[1, g] = targets_ref[g * own : (g + 1) * own, :]
    fixed_copies, half_copies, field_copies = [[], []], [], []

    def send_fixed(f):
        for k, peer in enumerate(peers):
            fixed_copies[f].append(
                send(fixed.at[f, peer], fixed_in.at[f, c], fixed_s.at[f, k], fixed_g.at[f, k], peer, h)
            )
        fixed_in[f, c] = fixed[f, c]

    pl.semaphore_wait(barrier, groups)
    send_fixed(0)

    def project(q):
        for p in range(2):
            rows = jnp.dot(
                x_ref[q * bite : (q + 1) * bite, :], w_ref[p], preferred_element_type=jnp.float32
            ).T
            for k in range(2 * groups):
                halves_out[q, k // groups, k % groups, p * own : (p + 1) * own, :] = rows[
                    k * own : (k + 1) * own, :
                ]

    project(0)

    def send_half(q):
        half_copies.append(
            send(halves_out.at[q, 1 - h], halves_in.at[q], half_s.at[q], half_g.at[q], c, 1 - h)
        )

    send_half(0)
    for q in range(1, BITES):
        project(q)
        send_half(q)
    for q in range(BITES):
        half_copies[q].wait_recv()
        fields[q] = halves_out[q, h] + halves_in[q]
        for k, peer in enumerate(peers):
            field_copies.append(
                send(fields.at[q, peer], fields_in.at[q, c], field_s.at[q, k], field_g.at[q, k], peer, h)
            )
        fields_in[q, c] = fields[q, c]
    send_fixed(1)

    mid_real, mid_imag = mid_ref[0], mid_ref[1]

    def gather(rows):
        return jnp.concatenate(
            [
                jnp.concatenate([row[:, s * LANES : (s + 1) * LANES] for row in rows], 1)
                for s in range(splits)
            ],
            0,
        )

    def spread(field, array):
        for i in range(own):
            for s in range(splits):
                back_out[field, :, i, s * LANES : (s + 1) * LANES] = array[
                    s * groups : (s + 1) * groups, i * LANES : (i + 1) * LANES
                ]

    def forward(array):
        stage = left_table(t1_ref, array)
        rows = []
        for i in range(own):
            real = stage[:coarse, i * LANES : (i + 1) * LANES]
            imag = stage[coarse:, i * LANES : (i + 1) * LANES]
            rows.append(
                jnp.concatenate(
                    [real * mid_real - imag * mid_imag, real * mid_imag + imag * mid_real], 1
                )
            )
        return right_table(jnp.concatenate(rows, 0), t2_ref)

    def backward(spectrum):
        stage = right_table(spectrum, t2i_ref)
        blocks = []
        for i in range(own):
            real = stage[i * coarse : (i + 1) * coarse, :LANES]
            imag = stage[i * coarse : (i + 1) * coarse, LANES:]
            blocks.append(
                jnp.concatenate(
                    [real * mid_real + imag * mid_imag, imag * mid_real - real * mid_imag], 0
                )
            )
        return left_table(t1i_ref, jnp.concatenate(blocks, 1))

    def times(left, right, sign):
        left_real, left_imag = left[:, :LANES], left[:, LANES:]
        right_real, right_imag = right[:, :LANES], sign * right[:, LANES:]
        return jnp.concatenate(
            [
                left_real * right_real - left_imag * right_imag,
                left_real * right_imag + left_imag * right_real,
            ],
            1,
        )

    def field(row):
        return jnp.concatenate([fields_in[q, :, row, :] for q in range(BITES)], 1)

    for copy in fixed_copies[0]:
        copy.wait_recv()
    filters = gather([fixed_in[0, :, i, :] for i in range(own)])
    skip = jnp.concatenate(
        [jnp.full((1, LANES), skip_ref[c * own + i], jnp.float32) for i in range(own)], 1
    )
    filter_spec = forward(filters)
    for copy in field_copies:
        copy.wait_recv()
    values = gather([field(i) for i in range(own)])
    gates = gather([field(own + i) for i in range(own)])
    value_spec = forward(values)
    conv = backward(times(value_spec, filter_spec, 1.0)) + skip * values
    outputs = gates * conv
    for copy in fixed_copies[1]:
        copy.wait_recv()
    targets = gather([fixed_in[1, :, i, :] for i in range(own)])
    residual = outputs - targets
    grad_conv = residual * gates

    def send_back(f, target):
        return [
            send(back_out.at[f, peer], target, back_s.at[f, k], back_g.at[f, k], peer, h)
            for k, peer in enumerate(peers)
        ]

    def relay(f, copies):
        flows = [send(back_in.at[f, h, c], back_in.at[f, h, c], relay_s.at[f, 0], relay_g.at[f, 0], c, 1 - h)]
        for k, source in enumerate(sources):
            copies[k].wait_recv()
            place = back_in.at[f, h, source]
            flows.append(send(place, place, relay_s.at[f, k + 1], relay_g.at[f, k + 1], c, 1 - h))
        return flows

    spread(1, residual * conv)
    back_in[1, h, c] = back_out[1, c]
    gate_copies = send_back(1, back_in.at[1, h, c])
    spread(2, outputs)
    grad_spec = forward(grad_conv)
    spread(0, backward(times(grad_spec, filter_spec, -1.0)) + skip * grad_conv)
    back_in[0, h, c] = back_out[0, c]
    value_copies = send_back(0, back_in.at[0, h, c])
    late = send_back(2, outputs_ref.at[c])
    flows = relay(1, gate_copies)
    spread(3, backward(times(grad_spec, value_spec, -1.0)) * scaling)
    value_flows = relay(0, value_copies)
    late += send_back(3, filter_ref.at[c])
    outputs_ref[c] = back_out[2, c]
    filter_ref[c] = back_out[3, c]

    width = columns // PIECES
    cuts = [pl.ds(j * width, width) for j in range(PIECES)]
    mid_z = far // 2
    crossings = {}

    def partial_rows(p, arrivals):
        for copy in arrivals:
            copy.wait_recv()
        for k in range(2 * groups):
            pair[p, k * own : (k + 1) * own, :] = back_in[p, k // groups, k % groups]
        high, low = split(pair[p])
        side = slice(p * mid_z, (p + 1) * mid_z)
        copies = []
        for j, cut in enumerate(cuts):
            piece = x_ref[:, cut]
            product_rows = jnp.dot(high, piece, preferred_element_type=jnp.float32) + jnp.dot(
                low, piece, preferred_element_type=jnp.float32
            )
            part[side, :, :, :, cut] = product_rows.reshape((mid_z,) + part.shape[1:-1] + (width,))
            span = pl.ds(p * mid_z, mid_z)
            copies.append(
                send(
                    part.at[span, :, 1 - core, :, cut], in1.at[span, :, :, cut],
                    s1.at[p, j], g1.at[p, j], core_peer, h,
                )
            )
        return copies

    def across_x(p, copies):
        side = slice(p * mid_z, (p + 1) * mid_z)
        span = pl.ds(p * mid_z, mid_z)
        onward = []
        for j, cut in enumerate(cuts):
            copies[j].wait_recv()
            sum1[side, :, :, cut] = part[side, :, core, :, cut] + in1[side, :, :, cut]
            onward.append(
                send(
                    sum1.at[span, 1 - x_side, :, cut], in2.at[span, :, cut],
                    s2.at[p, j], g2.at[p, j], x_peer, h,
                )
            )
        return onward

    def across_z(p, copies):
        side = slice(p * mid_z, (p + 1) * mid_z)
        for j, cut in enumerate(cuts):
            copies[j].wait_recv()
            sum2[side, :, cut] = sum1[side, x_side, :, cut] + in2[side, :, cut]
            for d, peer in enumerate(z_peers):
                place = peer // 4
                copy = pltpu.make_async_remote_copy(
                    src_ref=sum2.at[place, :, cut],
                    dst_ref=in3.at[d, :, cut],
                    send_sem=s3.at[j, d],
                    recv_sem=g3.at[j, d],
                    device_id=(peer, h),
                    device_id_type=MESH,
                )
                crossings[j, d] = copy
                pl.when(place // mid_z == p)(copy.start)

    gate_first = partial_rows(1, flows)
    gate_second = across_x(1, gate_first)
    value_first = partial_rows(0, value_flows)
    across_z(1, gate_second)
    value_second = across_x(0, value_first)
    high_ref[...], low_ref[...] = split(jnp.concatenate([pair[0].T, pair[1].T], 1))
    across_z(0, value_second)
    for j, cut in enumerate(cuts):
        total = sum2[z, :, cut]
        for d in range(far - 1):
            crossings[j, d].wait_recv()
            total = total + in3[d, :, cut]
        proj_ref[:, cut] = total * scaling
    sent.extend(crossings.values())
    for copy in late:
        copy.wait_recv()
    for copy in sent:
        copy.wait_send()


def final_kernel(
    high, low, w_ref, outs_ref, filt_ref, proj_ref, grad_ref, outputs_ref, filter_ref, grad_proj_ref
):
    groups, own, _ = outs_ref.shape

    @pl.when(pl.program_id(0) == 0)
    def _():
        grad_proj_ref[...] = proj_ref[...]
        for g in range(groups):
            outputs_ref[g * own : (g + 1) * own, :] = outs_ref[g]
            filter_ref[g * own : (g + 1) * own, :] = filt_ref[g]

    w = jnp.concatenate([w_ref[0], w_ref[1]], 1)
    flip = (((1,), (1,)), ((), ()))
    grad_ref[...] = lax.dot_general(
        high[...], w, flip, preferred_element_type=jnp.float32
    ) + lax.dot_general(low[...], w, flip, preferred_element_type=jnp.float32)


def per_device(inputs, proj_weight, filters, skip_gain, targets):
    groups, halves = lax.axis_size("ctx"), lax.axis_size("ch")
    frames, columns = inputs.shape
    channels = proj_weight.shape[2]
    own = channels // (groups * halves)
    fits = own * groups * halves == channels and own == 4 and groups % 16 == 0 and halves == 2
    if not fits or frames % (LANES * BITES) or columns % (LANES * PIECES):
        return general(inputs, proj_weight, filters, skip_gain, targets)
    length = frames * groups
    scaling = float(length) ** -0.5
    splits = frames // LANES
    t1, mid, t2, t2i, t1i = spectrum_tables(length // LANES, LANES)
    order = np.arange(length // LANES).reshape(groups, splits).T.reshape(-1)
    f32 = jnp.float32
    tables = [halves_of(table) for table in (t1[:, order], t2, t2i, t1i[order])]
    tables.insert(1, jnp.asarray(mid, f32))
    rows = 2 * channels // groups
    far = groups // 4
    vmem, dma = pltpu.VMEM, pltpu.SemaphoreType.DMA
    bite = frames // BITES
    blocks = jax.ShapeDtypeStruct((groups, own, frames), f32)
    outs, filt, high, low, proj = pl.pallas_call(
        functools.partial(main_kernel, own, scaling),
        out_shape=(
            blocks,
            blocks,
            jax.ShapeDtypeStruct((frames, 2 * channels), jnp.bfloat16),
            jax.ShapeDtypeStruct((frames, 2 * channels), jnp.bfloat16),
            jax.ShapeDtypeStruct((rows, columns), f32),
        ),
        in_specs=[VMEM_SPEC] * 4 + [pl.BlockSpec(memory_space=pltpu.SMEM)] + [VMEM_SPEC] * 5,
        out_specs=(VMEM_SPEC,) * 5,
        scratch_shapes=[
            vmem((2, groups, own, frames), f32),
            vmem((2, groups, own, frames), f32),
            vmem((BITES, 2, groups, 2 * own, bite), f32),
            vmem((BITES, groups, 2 * own, bite), f32),
            vmem((BITES, groups, 2 * own, bite), f32),
            vmem((BITES, groups, 2 * own, bite), f32),
            vmem((4, groups, own, frames), f32),
            vmem((2, 2, groups, own, frames), f32),
            vmem((2, channels, frames), f32),
            vmem((far, 2, 2, rows, columns), f32),
            vmem((far, 2, rows, columns), f32),
            vmem((far, 2, rows, columns), f32),
            vmem((far, rows, columns), f32),
            vmem((far, rows, columns), f32),
            vmem((far - 1, rows, columns), f32),
            dma((2, groups - 1)),
            dma((2, groups - 1)),
            dma((BITES,)),
            dma((BITES,)),
            dma((BITES, groups - 1)),
            dma((BITES, groups - 1)),
            dma((4, groups - 1)),
            dma((4, groups - 1)),
            dma((2, groups)),
            dma((2, groups)),
            dma((2, PIECES)),
            dma((2, PIECES)),
            dma((2, PIECES)),
            dma((2, PIECES)),
            dma((PIECES, far - 1)),
            dma((PIECES, far - 1)),
        ],
        compiler_params=pltpu.CompilerParams(
            collective_id=0, has_side_effects=True, vmem_limit_bytes=60 * 1024 * 1024
        ),
    )(inputs, proj_weight, filters, targets, skip_gain, *tables)

    def whole(*shape):
        return pl.BlockSpec(shape, lambda j: (0,) * len(shape))

    width = columns // 4
    grad_inputs, outputs, grad_filter, grad_proj = pl.pallas_call(
        final_kernel,
        grid=(4,),
        out_shape=(
            jax.ShapeDtypeStruct((frames, columns), f32),
            jax.ShapeDtypeStruct(filters.shape, f32),
            jax.ShapeDtypeStruct(filters.shape, f32),
            jax.ShapeDtypeStruct((rows, columns), f32),
        ),
        in_specs=[
            whole(frames, 2 * channels),
            whole(frames, 2 * channels),
            pl.BlockSpec((2, width, channels), lambda j: (0, j, 0)),
            whole(groups, own, frames),
            whole(groups, own, frames),
            whole(rows, columns),
        ],
        out_specs=(
            pl.BlockSpec((frames, width), lambda j: (0, j)),
            whole(*filters.shape),
            whole(*filters.shape),
            whole(rows, columns),
        ),
    )(high, low, proj_weight, outs, filt, proj)
    return outputs, grad_inputs, grad_filter, grad_proj


def solution(mesh):
    placed = (P("ctx", "ch"), P(None, "ch", None), P("ch", "ctx"), P("ch"), P("ch", "ctx"))
    return jax.shard_map(
        per_device,
        mesh=mesh,
        in_specs=placed,
        out_specs=(P("ch", "ctx"), P("ctx", "ch"), P("ch", "ctx"), P("ctx", "ch")),
        check_vma=False,
    )
```
